32 devices in a mesh: seq: 8 (over z, x), head: 4 (over y, core).
Axes of the slice: x: 2, y: 2, z: 4, core: 2. Of those that a mesh axis runs over, the one named last changes fastest.
Arguments:
- queries: bfloat16 [2, 1024, 2048], P(None, 'seq', 'head'), may hold values from -6 to 6
- keys: bfloat16 [2, 1024, 2048], P(None, 'seq', 'head'), may hold values from -6 to 6
- values: bfloat16 [2, 1024, 2048], P(None, 'seq', 'head'), may hold values from -6 to 6
- out_grad: bfloat16 [2, 1024, 2048], P(None, 'seq', 'head'), may hold values from -6 to 6
- out_gain: float32 [2, 2048], P(None, 'head'), may hold values from 0.5 to 1.5
Outputs:
- normed: bfloat16 [2, 1024, 2048], P(None, 'seq', 'head')
- grad_queries: bfloat16 [2, 1024, 2048], P(None, 'seq', 'head')
- grad_keys: bfloat16 [2, 1024, 2048], P(None, 'seq', 'head')
- grad_values: bfloat16 [2, 1024, 2048], P(None, 'seq', 'head')
The draws below stay inside these ranges and needn't reach their ends.
All inputs are finite; a program needn't handle non-finite values.
Results may differ from the reference program's by a relative error of at most 0.0058.
Values sent between devices are 32-bit elements; how exact they have to be, the bound alone decides.
No kernel may reach another device: no remote copies, remote signals or barrier semaphores. Data moves between devices by JAX's collectives and lax.ppermute only.
A program may use at most 192 MiB of HBM per device.

```python
import jax
import jax.numpy as jnp
from jax import lax

HEADS = 16
DH = 128
CH = 128
LAYERS = 2
SEQ = 1024
FEAT = 2048


def block_levels(key, dims, pieces, smallest, top_value):
    level, own = 1.0, jax.random.fold_in(key, 6)
    for dim, parts in pieces:
        draws = jnp.exp(jax.random.uniform(jax.random.fold_in(own, dim), (parts,), jnp.float32, smallest / len(pieces), top_value / len(pieces)))
        level = level * jnp.repeat(draws, dims[dim] // parts).reshape([-1 if axis == dim else 1 for axis in range(len(dims))])
    return level


def centred(own_key, dims, spread, limit, shards=(), kind=jnp.bfloat16):
    drawn = jax.random.normal(own_key, dims, jnp.float32) * spread
    if len(shards) > 0:
        drawn = block_levels(own_key, dims, shards, -0.22, 0.18) * drawn
    return jnp.clip(drawn, min=-limit, max=limit).astype(kind)


def setup_inputs(seed: int = 0) -> dict:
    seeds = jax.random.split(jax.random.key(seed), 6)
    queries = centred(seeds[0], (LAYERS, SEQ, FEAT), 1.0, 6.0, ((1, 8), (2, 4)))
    keys = centred(seeds[1], (LAYERS, SEQ, FEAT), 1.0, 6.0, ((1, 8), (2, 4)))
    values = centred(seeds[2], (LAYERS, SEQ, FEAT), 1.0, 6.0, ((1, 8), (2, 4)))
    out_grad = centred(seeds[3], (LAYERS, SEQ, FEAT), 1.0, 6.0, ((1, 8), (2, 4)))
    out_gain = jnp.clip(1.0 + 0.1 * jax.random.normal(seeds[4], (LAYERS, FEAT), jnp.float32), 0.5, 1.5)
    return dict(queries=queries, keys=keys, values=values, out_grad=out_grad, out_gain=out_gain)


EPSILON = 1e-06

def to_bf16(value):
    return lax.optimization_barrier(value.astype(jnp.bfloat16)).astype(jnp.float32)

def one_layer(query, key_part, value_part, grad_part, gain_row):
    blocks = SEQ // CH
    block_shape = (blocks, CH, HEADS, DH)
    q_blocks = query.astype(jnp.float32).reshape(block_shape)
    k_blocks = key_part.astype(jnp.float32).reshape(block_shape)
    v_blocks = value_part.astype(jnp.float32).reshape(block_shape)
    score_scale = DH ** (-0.5)
    rows_idx = lax.broadcasted_iota(jnp.int32, (CH, CH), 0)
    cols_idx = lax.broadcasted_iota(jnp.int32, (CH, CH), 1)
    causal = rows_idx >= cols_idx
    kv_blocks = jnp.einsum('bchd,bche->bhde', k_blocks, v_blocks)
    zero_block = jnp.zeros_like(kv_blocks[:1])
    state = jnp.cumsum(jnp.concatenate([zero_block, kv_blocks[:-1]], 0), 0)
    state16 = to_bf16(state)
    scores = jnp.einsum('bchd,bshd->bhcs', q_blocks, k_blocks) * score_scale
    attn_weights = to_bf16(jnp.where(causal, scores, 0.0))
    attn = score_scale * jnp.einsum('bchd,bhde->bche', q_blocks, state16) + jnp.einsum('bhcs,bshe->bche', attn_weights, v_blocks)
    attn = attn.reshape(SEQ, FEAT)
    root = jnp.sqrt(lax.optimization_barrier(jnp.mean(attn * attn, -1, keepdims=True)) + EPSILON)
    normed = (attn / root * gain_row[None, :]).astype(jnp.bfloat16)
    upper = gain_row[None, :] * grad_part.astype(jnp.float32)
    cross_sum = lax.optimization_barrier(jnp.sum(upper * attn, -1, keepdims=True)) / FEAT
    grad_attn = to_bf16(upper / root - attn * cross_sum / (root * root * root))
    g_blocks = grad_attn.reshape(block_shape)
    dweights = to_bf16(jnp.where(causal, jnp.einsum('bche,bshe->bhcs', g_blocks, v_blocks) * score_scale, 0.0))
    back_blocks = jnp.einsum('bchd,bche->bhde', q_blocks, g_blocks)
    later_sum = jnp.cumsum(back_blocks[::-1], 0)[::-1] - back_blocks
    back16 = to_bf16(score_scale * later_sum)
    grad_q = score_scale * jnp.einsum('bche,bhde->bchd', g_blocks, state16) + jnp.einsum('bhcs,bshd->bchd', dweights, k_blocks)
    grad_k = jnp.einsum('bche,bhde->bchd', v_blocks, back16) + jnp.einsum('bhcs,bchd->bshd', dweights, q_blocks)
    grad_v = jnp.einsum('bchd,bhde->bche', k_blocks, back16) + jnp.einsum('bhcs,bche->bshe', attn_weights, g_blocks)
    return (normed, grad_q.reshape(SEQ, FEAT).astype(jnp.bfloat16), grad_k.reshape(SEQ, FEAT).astype(jnp.bfloat16), grad_v.reshape(SEQ, FEAT).astype(jnp.bfloat16))

def reference(queries, keys, values, out_grad, out_gain):
    results = [one_layer(queries[layer], keys[layer], values[layer], out_grad[layer], out_gain[layer]) for layer in range(LAYERS)]
    normed = jnp.stack([item[0] for item in results])
    grad_queries = jnp.stack([item[1] for item in results])
    grad_keys = jnp.stack([item[2] for item in results])
    grad_values = jnp.stack([item[3] for item in results])
    return (normed, grad_queries, grad_keys, grad_values)
```

```python
import functools

import jax
import jax.numpy as jnp
from jax import lax
from jax.experimental import pallas as pl
from jax.experimental.pallas import tpu as pltpu
from jax.sharding import PartitionSpec as P

DH = 128
CH = 128
GROUP = 4

EPSILON = 1e-06
SCALE = DH ** (-0.5)
F32 = jnp.float32
BF16 = jnp.bfloat16


def dot(a, b, ca, cb):
    return lax.dot_general(a, b, (((ca,), (cb,)), ((), ())), preferred_element_type=F32)


def lanes(head):
    return pl.ds(pl.multiple_of(head * DH, DH), DH)


def causal_mask():
    rows = lax.broadcasted_iota(jnp.int32, (CH, CH), 0)
    cols = lax.broadcasted_iota(jnp.int32, (CH, CH), 1)
    return rows >= cols


def kv_kernel(place_ref, k_ref, v_ref, *outs):
    place = place_ref[0]
    for turn, out in enumerate(outs):
        at = lanes(lax.bitwise_xor(place, turn))
        for layer in range(k_ref.shape[0]):
            out[layer] = dot(k_ref[layer, :, at], v_ref[layer, :, at], 0, 0)


def local_kernel(q_ref, k_ref, v_ref, w_ref, loc_ref):
    mask = causal_mask()
    layers, _, width = q_ref.shape
    for layer in range(layers):
        for head in range(width // DH):
            at = pl.ds(head * DH, DH)
            scores = dot(q_ref[layer, :, at], k_ref[layer, :, at], 1, 1) * SCALE
            w = jnp.where(mask, scores, 0.0).astype(BF16)
            w_ref[layer, :, at] = w
            loc_ref[layer, :, at] = dot(w, v_ref[layer, :, at], 1, 0)


def attn_kernel(place_ref, q_ref, loc_ref, g_ref, gain_ref, *rest):
    states, (attn_ref, s16_ref, sums_ref) = rest[:GROUP], rest[GROUP:]
    place = place_ref[0]
    layers = q_ref.shape[0]
    lane = lax.broadcasted_iota(jnp.int32, (CH, CH), 1)
    columns = jnp.zeros((CH, CH), F32)
    for layer in range(layers):
        square = jnp.zeros((CH, DH), F32)
        cross = jnp.zeros((CH, DH), F32)
        for turn in range(GROUP):
            at = lanes(lax.bitwise_xor(place, turn))
            s16 = states[turn][layer].astype(BF16)
            s16_ref[layer, :, at] = s16
            attn = SCALE * dot(q_ref[layer, :, at], s16, 1, 0) + loc_ref[layer, :, at]
            attn_ref[layer, :, at] = attn
            upper = gain_ref[layer : layer + 1, at] * g_ref[layer, :, at].astype(F32)
            square += attn * attn
            cross += upper * attn
        columns += jnp.where(lane == 2 * layer, jnp.sum(square, 1, keepdims=True), 0.0)
        columns += jnp.where(lane == 2 * layer + 1, jnp.sum(cross, 1, keepdims=True), 0.0)
    sums_ref[...] = columns.T[: sums_ref.shape[0]]


def grad_kernel(total_width, place_ref, attn_ref, g_ref, gain_ref, q_ref, *rest):
    parts = rest[: len(rest) - GROUP - 2]
    normed_ref, ga_ref = rest[len(parts) : len(parts) + 2]
    outs = rest[len(parts) + 2 :]
    place = place_ref[0]
    layers = attn_ref.shape[0]
    sums = parts[0][...]
    for part in parts[1:]:
        sums = sums + part[...]
    sums = jnp.concatenate([sums, jnp.zeros((CH - sums.shape[0], CH), F32)], 0).T
    for layer in range(layers):
        square = sums[:, 2 * layer : 2 * layer + 1] * (1.0 / total_width)
        cross = sums[:, 2 * layer + 1 : 2 * layer + 2] * (1.0 / total_width)
        inv = 1.0 / jnp.sqrt(square + EPSILON)
        back = cross * (inv * inv * inv)
        for turn in range(GROUP):
            at = lanes(lax.bitwise_xor(place, turn))
            attn = attn_ref[layer, :, at]
            gain = gain_ref[layer : layer + 1, at]
            normed_ref[layer, :, at] = (attn * inv * gain).astype(BF16)
            upper = gain * g_ref[layer, :, at].astype(F32)
            ga = (upper * inv - attn * back).astype(BF16)
            ga_ref[layer, :, at] = ga
            outs[turn][layer] = dot(q_ref[layer, :, at], ga, 0, 0)


def inner_kernel(q_ref, k_ref, v_ref, ga_ref, s16_ref, w_ref, gq_ref, gkl_ref, gvl_ref):
    mask = causal_mask()
    layers, _, width = q_ref.shape
    for layer in range(layers):
        for head in range(width // DH):
            at = pl.ds(head * DH, DH)
            ga = ga_ref[layer, :, at]
            dscores = dot(ga, v_ref[layer, :, at], 1, 1) * SCALE
            dw = jnp.where(mask, dscores, 0.0).astype(BF16)
            gq = SCALE * dot(ga, s16_ref[layer, :, at], 1, 1)
            gq_ref[layer, :, at] = (gq + dot(dw, k_ref[layer, :, at], 1, 0)).astype(BF16)
            gkl_ref[layer, :, at] = dot(dw, q_ref[layer, :, at], 0, 0)
            gvl_ref[layer, :, at] = dot(w_ref[layer, :, at], ga, 0, 0)


def outer_kernel(place_ref, k_ref, v_ref, gkl_ref, gvl_ref, *rest):
    backs, (gk_ref, gv_ref) = rest[:GROUP], rest[GROUP:]
    place = place_ref[0]
    for layer in range(k_ref.shape[0]):
        for turn in range(GROUP):
            at = lanes(lax.bitwise_xor(place, turn))
            b16 = (SCALE * backs[turn][layer]).astype(BF16)
            gk = dot(v_ref[layer, :, at], b16, 1, 1) + gkl_ref[layer, :, at]
            gv = dot(k_ref[layer, :, at], b16, 1, 0) + gvl_ref[layer, :, at]
            gk_ref[layer, :, at] = gk.astype(BF16)
            gv_ref[layer, :, at] = gv.astype(BF16)


def call(body, outs, smem, flops, *args):
    moved = sum(a.size * a.dtype.itemsize for a in [*args, *outs])
    return pl.pallas_call(
        body,
        out_shape=outs,
        in_specs=[pl.BlockSpec(memory_space=pltpu.SMEM)] * smem
        + [pl.BlockSpec(memory_space=pltpu.VMEM)] * (len(args) - smem),
        out_specs=[pl.BlockSpec(memory_space=pltpu.VMEM)] * len(outs),
        cost_estimate=pl.CostEstimate(flops=flops, bytes_accessed=moved, transcendentals=0),
    )(*args)


def carried(chunks, place, count, reverse):
    def swap(array, turn):
        return lax.ppermute(array, "seq", [(i, i ^ turn) for i in range(count)])

    def shift(array, by):
        if reverse:
            pairs = [(i + by, i) for i in range(count - by)]
        else:
            pairs = [(i, i + by) for i in range(count - by)]
        return lax.ppermute(array, "seq", pairs)

    got = [chunks[0]] + [swap(chunks[t], t) for t in range(1, GROUP)]
    total = got[0] + got[1] + got[2] + got[3]
    outside = shift(total, GROUP)
    by = 1
    while by < count // GROUP - 1:
        outside = outside + shift(outside, by * GROUP)
        by *= 2
    results = []
    for turn in range(GROUP):
        goal = lax.bitwise_xor(place, turn)
        value = outside
        for t in range(GROUP):
            source = lax.bitwise_xor(place, t)
            reached = source > goal if reverse else source < goal
            value = value + jnp.where(reached, got[t], 0.0)
        results.append(value)
    return [results[0]] + [swap(results[t], t) for t in range(1, GROUP)]


def per_device(seq_count, head_count, queries, keys, values, out_grad, out_gain):
    layers, tok_rows, width = queries.shape
    heads = width // DH
    assert tok_rows == CH and heads == GROUP and seq_count % GROUP == 0
    assert 2 * layers <= 8
    place = lax.axis_index("seq") % GROUP
    place_arg = place.astype(jnp.int32).reshape(1)
    wide = lambda dtype: jax.ShapeDtypeStruct((layers, CH, width), dtype)
    blocks = [jax.ShapeDtypeStruct((layers, DH, DH), F32)] * GROUP
    product = 2 * layers * heads * CH * DH * DH

    kv = call(kv_kernel, blocks, 1, product, place_arg, keys, values)
    states = carried(kv, place, seq_count, False)
    weights, local = call(
        local_kernel, [wide(BF16), wide(F32)], 0, 2 * product, queries, keys, values
    )
    attn, s16, sums = call(
        attn_kernel,
        [wide(F32), wide(BF16), jax.ShapeDtypeStruct((8, CH), F32)],
        1,
        product,
        place_arg,
        queries,
        local,
        out_grad,
        out_gain,
        *states,
    )
    parts = [sums] + [
        lax.ppermute(sums, "head", [(i, (i + by) % head_count) for i in range(head_count)])
        for by in range(1, head_count)
    ]
    normed, ga, *products = call(
        functools.partial(grad_kernel, width * head_count),
        [wide(BF16), wide(BF16), *blocks],
        1,
        product,
        place_arg,
        attn,
        out_grad,
        out_gain,
        queries,
        *parts,
    )
    later = carried(products, place, seq_count, True)
    grad_q, gk_local, gv_local = call(
        inner_kernel,
        [wide(BF16), wide(F32), wide(F32)],
        0,
        5 * product,
        queries,
        keys,
        values,
        ga,
        s16,
        weights,
    )
    grad_k, grad_v = call(
        outer_kernel,
        [wide(BF16), wide(BF16)],
        1,
        2 * product,
        place_arg,
        keys,
        values,
        gk_local,
        gv_local,
        *later,
    )
    return normed, grad_q, grad_k, grad_v


def solution(mesh):
    block = P(None, "seq", "head")
    return jax.shard_map(
        functools.partial(per_device, mesh.shape["seq"], mesh.shape["head"]),
        mesh=mesh,
        in_specs=(block, block, block, block, P(None, "head")),
        out_specs=(block, block, block, block),
        check_vma=False,
    )
```

```python
import functools

import jax
import jax.numpy as jnp
from jax import lax
from jax.experimental import pallas as pl
from jax.experimental.pallas import tpu as pltpu
from jax.sharding import PartitionSpec as P

DH = 128
CH = 128
GROUP = 4

EPSILON = 1e-06
SCALE = DH ** (-0.5)
F32 = jnp.float32
BF16 = jnp.bfloat16


def dot(a, b, ca, cb):
    return lax.dot_general(a, b, (((ca,), (cb,)), ((), ())), preferred_element_type=F32)


def lanes(head):
    return pl.ds(pl.multiple_of(head * DH, DH), DH)


def causal_mask():
    rows = lax.broadcasted_iota(jnp.int32, (CH, CH), 0)
    cols = lax.broadcasted_iota(jnp.int32, (CH, CH), 1)
    return rows >= cols


def kv_kernel(place_ref, k_ref, v_ref, *outs):
    place = place_ref[0]
    for turn, out in enumerate(outs):
        at = lanes(lax.bitwise_xor(place, turn))
        for layer in range(k_ref.shape[0]):
            out[layer] = dot(k_ref[layer, :, at], v_ref[layer, :, at], 0, 0)


def local_kernel(q_ref, k_ref, v_ref, w_ref, loc_ref):
    mask = causal_mask()
    layers, _, width = q_ref.shape
    for layer in range(layers):
        for head in range(width // DH):
            at = pl.ds(head * DH, DH)
            scores = dot(q_ref[layer, :, at], k_ref[layer, :, at], 1, 1) * SCALE
            w = jnp.where(mask, scores, 0.0).astype(BF16)
            w_ref[layer, :, at] = w
            loc_ref[layer, :, at] = dot(w, v_ref[layer, :, at], 1, 0)


def attn_kernel(place_ref, q_ref, loc_ref, g_ref, gain_ref, *rest):
    states, (attn_ref, s16_ref, sums_ref) = rest[:GROUP], rest[GROUP:]
    place = place_ref[0]
    layers = q_ref.shape[0]
    lane = lax.broadcasted_iota(jnp.int32, (CH, CH), 1)
    columns = jnp.zeros((CH, CH), F32)
    for layer in range(layers):
        square = jnp.zeros((CH, DH), F32)
        cross = jnp.zeros((CH, DH), F32)
        for turn in range(GROUP):
            at = lanes(lax.bitwise_xor(place, turn))
            s16 = states[turn][layer].astype(BF16)
            s16_ref[layer, :, at] = s16
            attn = SCALE * dot(q_ref[layer, :, at], s16, 1, 0) + loc_ref[layer, :, at]
            attn_ref[layer, :, at] = attn
            upper = gain_ref[layer : layer + 1, at] * g_ref[layer, :, at].astype(F32)
            square += attn * attn
            cross += upper * attn
        columns += jnp.where(lane == 2 * layer, jnp.sum(square, 1, keepdims=True), 0.0)
        columns += jnp.where(lane == 2 * layer + 1, jnp.sum(cross, 1, keepdims=True), 0.0)
    sums_ref[...] = columns.T[: sums_ref.shape[0]]


def grad_kernel(total_width, place_ref, attn_ref, g_ref, gain_ref, q_ref, *rest):
    parts = rest[: len(rest) - GROUP - 2]
    normed_ref, ga_ref = rest[len(parts) : len(parts) + 2]
    outs = rest[len(parts) + 2 :]
    place = place_ref[0]
    layers = attn_ref.shape[0]
    sums = parts[0][...]
    for part in parts[1:]:
        sums = sums + part[...]
    sums = jnp.concatenate([sums, jnp.zeros((CH - sums.shape[0], CH), F32)], 0).T
    for layer in range(layers):
        square = sums[:, 2 * layer : 2 * layer + 1] * (1.0 / total_width)
        cross = sums[:, 2 * layer + 1 : 2 * layer + 2] * (1.0 / total_width)
        inv = 1.0 / jnp.sqrt(square + EPSILON)
        back = cross * (inv * inv * inv)
        for turn in range(GROUP):
            at = lanes(lax.bitwise_xor(place, turn))
            attn = attn_ref[layer, :, at]
            gain = gain_ref[layer : layer + 1, at]
            normed_ref[layer, :, at] = (attn * inv * gain).astype(BF16)
            upper = gain * g_ref[layer, :, at].astype(F32)
            ga = (upper * inv - attn * back).astype(BF16)
            ga_ref[layer, :, at] = ga
            outs[turn][layer] = dot(q_ref[layer, :, at], ga, 0, 0)


def inner_kernel(q_ref, k_ref, v_ref, ga_ref, s16_ref, w_ref, gq_ref, gkl_ref, gvl_ref):
    mask = causal_mask()
    layers, _, width = q_ref.shape
    for layer in range(layers):
        for head in range(width // DH):
            at = pl.ds(head * DH, DH)
            ga = ga_ref[layer, :, at]
            dscores = dot(ga, v_ref[layer, :, at], 1, 1) * SCALE
            dw = jnp.where(mask, dscores, 0.0).astype(BF16)
            gq = SCALE * dot(ga, s16_ref[layer, :, at], 1, 1)
            gq_ref[layer, :, at] = (gq + dot(dw, k_ref[layer, :, at], 1, 0)).astype(BF16)
            gkl_ref[layer, :, at] = dot(dw, q_ref[layer, :, at], 0, 0)
            gvl_ref[layer, :, at] = dot(w_ref[layer, :, at], ga, 0, 0)


def outer_kernel(place_ref, k_ref, v_ref, gkl_ref, gvl_ref, *rest):
    backs, (gk_ref, gv_ref) = rest[:GROUP], rest[GROUP:]
    place = place_ref[0]
    for layer in range(k_ref.shape[0]):
        for turn in range(GROUP):
            at = lanes(lax.bitwise_xor(place, turn))
            b16 = (SCALE * backs[turn][layer]).astype(BF16)
            gk = dot(v_ref[layer, :, at], b16, 1, 1) + gkl_ref[layer, :, at]
            gv = dot(k_ref[layer, :, at], b16, 1, 0) + gvl_ref[layer, :, at]
            gk_ref[layer, :, at] = gk.astype(BF16)
            gv_ref[layer, :, at] = gv.astype(BF16)


def call(body, outs, smem, flops, *args, hbm=()):
    moved = sum(a.size * a.dtype.itemsize for a in [*args, *outs])
    args = args[:smem] + tuple(
        pltpu.with_memory_space_constraint(a, pltpu.VMEM) for a in args[smem:]
    )
    return pl.pallas_call(
        body,
        out_shape=[a if i in hbm else pltpu.VMEM(a.shape, a.dtype) for i, a in enumerate(outs)],
        compiler_params=pltpu.CompilerParams(vmem_limit_bytes=4 * 2**20),
        in_specs=[pl.BlockSpec(memory_space=pltpu.SMEM)] * smem
        + [pl.BlockSpec(memory_space=pltpu.VMEM)] * (len(args) - smem),
        out_specs=[pl.BlockSpec(memory_space=pltpu.VMEM)] * len(outs),
        cost_estimate=pl.CostEstimate(flops=flops, bytes_accessed=moved, transcendentals=0),
    )(*args)


def carried(chunks, place, count, reverse):
    def swap(array, turn):
        return lax.ppermute(array, "seq", [(i, i ^ turn) for i in range(count)])

    def shift(array, by):
        if reverse:
            pairs = [(i + by, i) for i in range(count - by)]
        else:
            pairs = [(i, i + by) for i in range(count - by)]
        return lax.ppermute(array, "seq", pairs)

    got = [chunks[0]] + [swap(chunks[t], t) for t in range(1, GROUP)]
    total = got[0] + got[1] + got[2] + got[3]
    outside = shift(total, GROUP)
    by = 1
    while by < count // GROUP - 1:
        outside = outside + shift(outside, by * GROUP)
        by *= 2
    results = []
    for turn in range(GROUP):
        goal = lax.bitwise_xor(place, turn)
        value = outside
        for t in range(GROUP):
            source = lax.bitwise_xor(place, t)
            reached = source > goal if reverse else source < goal
            value = value + jnp.where(reached, got[t], 0.0)
        results.append(value)
    return [results[0]] + [swap(results[t], t) for t in range(1, GROUP)]


def per_device(seq_count, head_count, queries, keys, values, out_grad, out_gain):
    layers, tok_rows, width = queries.shape
    heads = width // DH
    assert tok_rows == CH and heads == GROUP and seq_count % GROUP == 0
    assert 2 * layers <= 8
    place = lax.axis_index("seq") % GROUP
    place_arg = place.astype(jnp.int32).reshape(1)
    wide = lambda dtype: jax.ShapeDtypeStruct((layers, CH, width), dtype)
    blocks = [jax.ShapeDtypeStruct((layers, DH, DH), F32)] * GROUP
    product = 2 * layers * heads * CH * DH * DH

    kv = call(kv_kernel, blocks, 1, product, place_arg, keys, values)
    states = carried(kv, place, seq_count, False)
    weights, local = call(
        local_kernel, [wide(BF16), wide(F32)], 0, 2 * product, queries, keys, values
    )
    attn, s16, sums = call(
        attn_kernel,
        [wide(F32), wide(BF16), jax.ShapeDtypeStruct((8, CH), F32)],
        1,
        product,
        place_arg,
        queries,
        local,
        out_grad,
        out_gain,
        *states,
    )
    parts = [sums] + [
        lax.ppermute(sums, "head", [(i, (i + by) % head_count) for i in range(head_count)])
        for by in range(1, head_count)
    ]
    normed, ga, *products = call(
        functools.partial(grad_kernel, width * head_count),
        [wide(BF16), wide(BF16), *blocks],
        1,
        product,
        place_arg,
        attn,
        out_grad,
        out_gain,
        queries,
        *parts,
        hbm=(0,),
    )
    later = carried(products, place, seq_count, True)
    grad_q, gk_local, gv_local = call(
        inner_kernel,
        [wide(BF16), wide(F32), wide(F32)],
        0,
        5 * product,
        queries,
        keys,
        values,
        ga,
        s16,
        weights,
        hbm=(0,),
    )
    grad_k, grad_v = call(
        outer_kernel,
        [wide(BF16), wide(BF16)],
        1,
        2 * product,
        place_arg,
        keys,
        values,
        gk_local,
        gv_local,
        *later,
        hbm=(0, 1),
    )
    return normed, grad_q, grad_k, grad_v


def solution(mesh):
    block = P(None, "seq", "head")
    return jax.shard_map(
        functools.partial(per_device, mesh.shape["seq"], mesh.shape["head"]),
        mesh=mesh,
        in_specs=(block, block, block, block, P(None, "head")),
        out_specs=(block, block, block, block),
        check_vma=False,
    )
```

```python
import functools

import jax
import jax.numpy as jnp
from jax import lax
from jax.experimental import pallas as pl
from jax.experimental.pallas import tpu as pltpu
from jax.sharding import PartitionSpec as P

DH = 128
CH = 128
GROUP = 4
ORDERS = ((1, 2, 3), (3, 2, 1), (1, 2, 3), (3, 2, 1))
CYCLIC = True
BARRIER = False
AR = (3, 2, 1)
RING = True

EPSILON = 1e-06
SCALE = DH ** (-0.5)
F32 = jnp.float32
BF16 = jnp.bfloat16


def dot(a, b, ca, cb):
    return lax.dot_general(a, b, (((ca,), (cb,)), ((), ())), preferred_element_type=F32)


def lanes(head):
    return pl.ds(pl.multiple_of(head * DH, DH), DH)


def causal_mask():
    rows = lax.broadcasted_iota(jnp.int32, (CH, CH), 0)
    cols = lax.broadcasted_iota(jnp.int32, (CH, CH), 1)
    return rows >= cols


def kv_kernel(order, place_ref, k_ref, v_ref, *outs):
    place = place_ref[0]
    for turn, out in zip((0, *order), outs):
        at = lanes(lax.bitwise_xor(place, turn))
        for layer in range(k_ref.shape[0]):
            out[layer] = dot(k_ref[layer, :, at], v_ref[layer, :, at], 0, 0)


def local_kernel(q_ref, k_ref, v_ref, w_ref, loc_ref):
    mask = causal_mask()
    layers, _, width = q_ref.shape
    for layer in range(layers):
        for head in range(width // DH):
            at = pl.ds(head * DH, DH)
            scores = dot(q_ref[layer, :, at], k_ref[layer, :, at], 1, 1) * SCALE
            w = jnp.where(mask, scores, 0.0).astype(BF16)
            w_ref[layer, :, at] = w
            loc_ref[layer, :, at] = dot(w, v_ref[layer, :, at], 1, 0)


def spread_kernel(reverse, order, order_back, place_ref, outside_ref, *refs):
    got, outs = refs[:GROUP], refs[GROUP:]
    place = place_ref[0]
    for layer in range(outside_ref.shape[0]):
        for turn, out in zip((0, *order_back), outs):
            goal = lax.bitwise_xor(place, turn)
            value = outside_ref[layer]
            for t, ref in zip((0, *order), got):
                source = lax.bitwise_xor(place, t)
                reached = source > goal if reverse else source < goal
                value = value + jnp.where(reached, ref[layer], 0.0)
            out[layer] = value


def attn_kernel(order, place_ref, q_ref, loc_ref, g_ref, gain_ref, *rest):
    states, (attn_ref, s16_ref, sums_ref) = rest[:GROUP], rest[GROUP:]
    place = place_ref[0]
    layers = q_ref.shape[0]
    lane = lax.broadcasted_iota(jnp.int32, (CH, CH), 1)
    columns = jnp.zeros((CH, CH), F32)
    for layer in range(layers):
        square = jnp.zeros((CH, DH), F32)
        cross = jnp.zeros((CH, DH), F32)
        for turn, state in zip((0, *order), states):
            at = lanes(lax.bitwise_xor(place, turn))
            s16 = state[layer].astype(BF16)
            s16_ref[layer, :, at] = s16
            attn = SCALE * dot(q_ref[layer, :, at], s16, 1, 0) + loc_ref[layer, :, at]
            attn_ref[layer, :, at] = attn
            upper = gain_ref[layer : layer + 1, at] * g_ref[layer, :, at].astype(F32)
            square += attn * attn
            cross += upper * attn
        columns += jnp.where(lane == 2 * layer, jnp.sum(square, 1, keepdims=True), 0.0)
        columns += jnp.where(lane == 2 * layer + 1, jnp.sum(cross, 1, keepdims=True), 0.0)
    sums_ref[...] = columns.T[: sums_ref.shape[0]]


def grad_kernel(total_width, order, place_ref, attn_ref, g_ref, gain_ref, q_ref, *rest):
    parts = rest[: len(rest) - GROUP - 2]
    ga_ref, inv_ref = rest[len(parts) : len(parts) + 2]
    outs = rest[len(parts) + 2 :]
    place = place_ref[0]
    layers = attn_ref.shape[0]
    sums = parts[0][...]
    for part in parts[1:]:
        sums = sums + part[...]
    sums = jnp.concatenate([sums, jnp.zeros((CH - sums.shape[0], CH), F32)], 0).T
    for layer in range(layers):
        square = sums[:, 2 * layer : 2 * layer + 1] * (1.0 / total_width)
        cross = sums[:, 2 * layer + 1 : 2 * layer + 2] * (1.0 / total_width)
        inv = 1.0 / jnp.sqrt(square + EPSILON)
        back = cross * (inv * inv * inv)
        inv_ref[layer] = jnp.broadcast_to(inv, inv_ref.shape[1:])
        for turn, out in zip((0, *order), outs):
            at = lanes(lax.bitwise_xor(place, turn))
            upper = gain_ref[layer : layer + 1, at] * g_ref[layer, :, at].astype(F32)
            ga = (upper * inv - attn_ref[layer, :, at] * back).astype(BF16)
            ga_ref[layer, :, at] = ga
            out[layer] = dot(q_ref[layer, :, at], ga, 0, 0)


def inner_kernel(q_ref, k_ref, v_ref, gain_ref, attn_ref, inv_ref, *rest):
    ga_ref, s16_ref, w_ref, normed_ref, gq_ref, gkl_ref, gvl_ref = rest
    mask = causal_mask()
    layers, _, width = q_ref.shape
    for layer in range(layers):
        for head in range(width // DH):
            at = pl.ds(head * DH, DH)
            gain = gain_ref[layer : layer + 1, at]
            normed_ref[layer, :, at] = (attn_ref[layer, :, at] * inv_ref[layer] * gain).astype(BF16)
            ga = ga_ref[layer, :, at]
            dscores = dot(ga, v_ref[layer, :, at], 1, 1) * SCALE
            dw = jnp.where(mask, dscores, 0.0).astype(BF16)
            gq = SCALE * dot(ga, s16_ref[layer, :, at], 1, 1)
            gq_ref[layer, :, at] = (gq + dot(dw, k_ref[layer, :, at], 1, 0)).astype(BF16)
            gkl_ref[layer, :, at] = dot(dw, q_ref[layer, :, at], 0, 0)
            gvl_ref[layer, :, at] = dot(w_ref[layer, :, at], ga, 0, 0)


def outer_kernel(order, place_ref, k_ref, v_ref, gkl_ref, gvl_ref, *rest):
    backs, (gk_ref, gv_ref) = rest[:GROUP], rest[GROUP:]
    place = place_ref[0]
    for layer in range(k_ref.shape[0]):
        for turn, back in zip((0, *order), backs):
            at = lanes(lax.bitwise_xor(place, turn))
            b16 = (SCALE * back[layer]).astype(BF16)
            gk = dot(v_ref[layer, :, at], b16, 1, 1) + gkl_ref[layer, :, at]
            gv = dot(k_ref[layer, :, at], b16, 1, 0) + gvl_ref[layer, :, at]
            gk_ref[layer, :, at] = gk.astype(BF16)
            gv_ref[layer, :, at] = gv.astype(BF16)


def call(body, outs, smem, flops, *args, hbm=()):
    moved = sum(a.size * a.dtype.itemsize for a in [*args, *outs])
    args = args[:smem] + tuple(
        pltpu.with_memory_space_constraint(a, pltpu.VMEM) for a in args[smem:]
    )
    return pl.pallas_call(
        body,
        out_shape=[a if i in hbm else pltpu.VMEM(a.shape, a.dtype) for i, a in enumerate(outs)],
        compiler_params=pltpu.CompilerParams(vmem_limit_bytes=4 * 2**20),
        in_specs=[pl.BlockSpec(memory_space=pltpu.SMEM)] * smem
        + [pl.BlockSpec(memory_space=pltpu.VMEM)] * (len(args) - smem),
        out_specs=[pl.BlockSpec(memory_space=pltpu.VMEM)] * len(outs),
        cost_estimate=pl.CostEstimate(flops=flops, bytes_accessed=moved, transcendentals=0),
    )(*args)


def carried(chunks, place, count, reverse, beside, order, order_back):
    def swap(array, turn):
        return lax.ppermute(array, "seq", [(i, i ^ turn) for i in range(count)])

    def shift(array, by):
        if CYCLIC:
            step = -by if reverse else by
            moved = lax.ppermute(array, "seq", [(i, (i + step) % count) for i in range(count)])
            inside = place < count - by if reverse else place >= by
            return jnp.where(inside, moved, 0.0)
        pairs = [(i, i + by) for i in range(count - by)]
        if reverse:
            pairs = [(b, a) for a, b in pairs]
        return lax.ppermute(array, "seq", pairs)

    got = [chunks[0]] + [swap(chunks[1 + j], t) for j, t in enumerate(order)]
    extra = beside()
    if BARRIER:
        got, extra = lax.optimization_barrier((got, extra))
    total = got[0] + got[1] + got[2] + got[3]
    outside = shift(total, GROUP)
    by = 1
    while by < count // GROUP - 1:
        outside = outside + shift(outside, by * GROUP)
        by *= 2
    own = lax.bitwise_and(place, GROUP - 1).astype(jnp.int32).reshape(1)
    results = call(
        functools.partial(spread_kernel, reverse, order, order_back),
        [jax.ShapeDtypeStruct(total.shape, F32)] * GROUP,
        1,
        0,
        own,
        outside,
        *got,
    )
    return [results[0]] + [swap(results[1 + j], t) for j, t in enumerate(order_back)], extra


def per_device(seq_count, head_count, queries, keys, values, out_grad, out_gain):
    layers, tok_rows, width = queries.shape
    heads = width // DH
    assert tok_rows == CH and heads == GROUP and seq_count % GROUP == 0
    assert 2 * layers <= 8
    place = lax.axis_index("seq")
    place_arg = lax.bitwise_and(place, GROUP - 1).astype(jnp.int32).reshape(1)
    wide = lambda dtype: jax.ShapeDtypeStruct((layers, CH, width), dtype)
    blocks = [jax.ShapeDtypeStruct((layers, DH, DH), F32)] * GROUP
    product = 2 * layers * heads * CH * DH * DH

    kv = call(functools.partial(kv_kernel, ORDERS[0]), blocks, 1, product, place_arg, keys, values)
    states, (weights, local) = carried(
        kv,
        place,
        seq_count,
        False,
        lambda: call(
            local_kernel, [wide(BF16), wide(F32)], 0, 2 * product, queries, keys, values
        ),
        ORDERS[0],
        ORDERS[1],
    )
    attn, s16, sums = call(
        functools.partial(attn_kernel, ORDERS[1]),
        [wide(F32), wide(BF16), jax.ShapeDtypeStruct((8, CH), F32)],
        1,
        product,
        place_arg,
        queries,
        local,
        out_grad,
        out_gain,
        *states,
    )
    parts = [sums] + [
        lax.ppermute(sums, "head", [(i, (i + by) % head_count if RING else i ^ by) for i in range(head_count)])
        for by in AR
    ]
    ga, inv, *products = call(
        functools.partial(grad_kernel, width * head_count, ORDERS[2]),
        [wide(BF16), jax.ShapeDtypeStruct((layers, CH, DH), F32), *blocks],
        1,
        product,
        place_arg,
        attn,
        out_grad,
        out_gain,
        queries,
        *parts,
    )
    later, (normed, grad_q, gk_local, gv_local) = carried(
        products,
        place,
        seq_count,
        True,
        lambda: call(
            inner_kernel,
            [wide(BF16), wide(BF16), wide(F32), wide(F32)],
            0,
            5 * product,
            queries,
            keys,
            values,
            out_gain,
            attn,
            inv,
            ga,
            s16,
            weights,
            hbm=(0, 1),
        ),
        ORDERS[2],
        ORDERS[3],
    )
    grad_k, grad_v = call(
        functools.partial(outer_kernel, ORDERS[3]),
        [wide(BF16), wide(BF16)],
        1,
        2 * product,
        place_arg,
        keys,
        values,
        gk_local,
        gv_local,
        *later,
        hbm=(0, 1),
    )
    return normed, grad_q, grad_k, grad_v


def solution(mesh):
    block = P(None, "seq", "head")
    return jax.shard_map(
        functools.partial(per_device, mesh.shape["seq"], mesh.shape["head"]),
        mesh=mesh,
        in_specs=(block, block, block, block, P(None, "head")),
        out_specs=(block, block, block, block),
        check_vma=False,
    )
```

```python
import functools

import jax
import jax.numpy as jnp
from jax import lax
from jax.experimental import pallas as pl
from jax.experimental.pallas import tpu as pltpu
from jax.sharding import PartitionSpec as P

DH = 128
CH = 128
GROUP = 4
ORDERS = ((2, 1, 3), (3, 1, 2), (1, 3, 2), (3, 1, 2))

EPSILON = 1e-06
SCALE = DH ** (-0.5)
F32 = jnp.float32
BF16 = jnp.bfloat16


def dot(a, b, ca, cb):
    return lax.dot_general(a, b, (((ca,), (cb,)), ((), ())), preferred_element_type=F32)


def lanes(head):
    return pl.ds(pl.multiple_of(head * DH, DH), DH)


def causal_mask():
    rows = lax.broadcasted_iota(jnp.int32, (CH, CH), 0)
    cols = lax.broadcasted_iota(jnp.int32, (CH, CH), 1)
    return rows >= cols


def kv_kernel(order, place_ref, k_hbm, v_hbm, k_ref, v_ref, *rest):
    outs, sems = rest[:GROUP], rest[GROUP]
    loads = [
        pltpu.make_async_copy(src.at[layer], dst.at[layer], sems.at[i, layer])
        for layer in range(k_ref.shape[0])
        for i, (src, dst) in enumerate(((k_hbm, k_ref), (v_hbm, v_ref)))
    ]
    for load in loads:
        load.start()
    for load in loads:
        load.wait()
    place = place_ref[0]
    for turn, out in zip((0, *order), outs):
        at = lanes(lax.bitwise_xor(place, turn))
        for layer in range(k_ref.shape[0]):
            out[layer] = dot(k_ref[layer, :, at], v_ref[layer, :, at], 0, 0)


def local_kernel(q_ref, k_ref, v_ref, w_ref, loc_ref):
    mask = causal_mask()
    layers, _, width = q_ref.shape
    for layer in range(layers):
        for head in range(width // DH):
            at = pl.ds(head * DH, DH)
            scores = dot(q_ref[layer, :, at], k_ref[layer, :, at], 1, 1) * SCALE
            w = jnp.where(mask, scores, 0.0).astype(BF16)
            w_ref[layer, :, at] = w
            loc_ref[layer, :, at] = dot(w, v_ref[layer, :, at], 1, 0)


def spread_kernel(reverse, order, order_back, place_ref, outside_ref, *refs):
    got, outs = refs[:GROUP], refs[GROUP:]
    place = place_ref[0]
    for layer in range(outside_ref.shape[0]):
        for turn, out in zip((0, *order_back), outs):
            goal = lax.bitwise_xor(place, turn)
            value = outside_ref[layer]
            for t, ref in zip((0, *order), got):
                source = lax.bitwise_xor(place, t)
                reached = source > goal if reverse else source < goal
                value = value + jnp.where(reached, ref[layer], 0.0)
            out[layer] = value


def attn_kernel(order, place_ref, q_ref, loc_ref, g_ref, gain_ref, *rest):
    states, (attn_ref, s16_ref, sums_ref) = rest[:GROUP], rest[GROUP:]
    place = place_ref[0]
    layers = q_ref.shape[0]
    lane = lax.broadcasted_iota(jnp.int32, (CH, CH), 1)
    columns = jnp.zeros((CH, CH), F32)
    for layer in range(layers):
        square = jnp.zeros((CH, DH), F32)
        cross = jnp.zeros((CH, DH), F32)
        for turn, state in zip((0, *order), states):
            at = lanes(lax.bitwise_xor(place, turn))
            s16 = state[layer].astype(BF16)
            s16_ref[layer, :, at] = s16
            attn = SCALE * dot(q_ref[layer, :, at], s16, 1, 0) + loc_ref[layer, :, at]
            attn_ref[layer, :, at] = attn
            upper = gain_ref[layer : layer + 1, at] * g_ref[layer, :, at].astype(F32)
            square += attn * attn
            cross += upper * attn
        columns += jnp.where(lane == 2 * layer, jnp.sum(square, 1, keepdims=True), 0.0)
        columns += jnp.where(lane == 2 * layer + 1, jnp.sum(cross, 1, keepdims=True), 0.0)
    sums_ref[...] = columns.T[: sums_ref.shape[0]]


def grad_kernel(total_width, order, place_ref, attn_ref, g_ref, gain_ref, q_ref, *rest):
    parts = rest[: len(rest) - GROUP - 2]
    ga_ref, inv_ref = rest[len(parts) : len(parts) + 2]
    outs = rest[len(parts) + 2 :]
    place = place_ref[0]
    layers = attn_ref.shape[0]
    sums = parts[0][...]
    for part in parts[1:]:
        sums = sums + part[...]
    sums = jnp.concatenate([sums, jnp.zeros((CH - sums.shape[0], CH), F32)], 0).T
    for layer in range(layers):
        square = sums[:, 2 * layer : 2 * layer + 1] * (1.0 / total_width)
        cross = sums[:, 2 * layer + 1 : 2 * layer + 2] * (1.0 / total_width)
        inv = 1.0 / jnp.sqrt(square + EPSILON)
        back = cross * (inv * inv * inv)
        inv_ref[layer] = jnp.broadcast_to(inv, inv_ref.shape[1:])
        for turn, out in zip((0, *order), outs):
            at = lanes(lax.bitwise_xor(place, turn))
            upper = gain_ref[layer : layer + 1, at] * g_ref[layer, :, at].astype(F32)
            ga = (upper * inv - attn_ref[layer, :, at] * back).astype(BF16)
            ga_ref[layer, :, at] = ga
            out[layer] = dot(q_ref[layer, :, at], ga, 0, 0)


def inner_kernel(q_ref, k_ref, v_ref, gain_ref, attn_ref, inv_ref, *rest):
    ga_ref, s16_ref, w_ref, normed_ref, gq_ref, gkl_ref, gvl_ref = rest
    mask = causal_mask()
    layers, _, width = q_ref.shape
    for layer in range(layers):
        for head in range(width // DH):
            at = pl.ds(head * DH, DH)
            gain = gain_ref[layer : layer + 1, at]
            normed_ref[layer, :, at] = (attn_ref[layer, :, at] * inv_ref[layer] * gain).astype(BF16)
            ga = ga_ref[layer, :, at]
            dscores = dot(ga, v_ref[layer, :, at], 1, 1) * SCALE
            dw = jnp.where(mask, dscores, 0.0).astype(BF16)
            gq = SCALE * dot(ga, s16_ref[layer, :, at], 1, 1)
            gq_ref[layer, :, at] = (gq + dot(dw, k_ref[layer, :, at], 1, 0)).astype(BF16)
            gkl_ref[layer, :, at] = dot(dw, q_ref[layer, :, at], 0, 0)
            gvl_ref[layer, :, at] = dot(w_ref[layer, :, at], ga, 0, 0)


def outer_kernel(order, place_ref, k_ref, v_ref, gkl_ref, gvl_ref, *rest):
    backs, (gk_hbm, gv_hbm, gk_ref, gv_ref, sems) = rest[:GROUP], rest[GROUP:]
    place = place_ref[0]
    stores = []
    for layer in range(k_ref.shape[0]):
        for turn, back in zip((0, *order), backs):
            at = lanes(lax.bitwise_xor(place, turn))
            b16 = (SCALE * back[layer]).astype(BF16)
            gk = dot(v_ref[layer, :, at], b16, 1, 1) + gkl_ref[layer, :, at]
            gv = dot(k_ref[layer, :, at], b16, 1, 0) + gvl_ref[layer, :, at]
            gk_ref[layer, :, at] = gk.astype(BF16)
            gv_ref[layer, :, at] = gv.astype(BF16)
        for i, (src, dst) in enumerate(((gk_ref, gk_hbm), (gv_ref, gv_hbm))):
            store = pltpu.make_async_copy(src.at[layer], dst.at[layer], sems.at[i, layer])
            store.start()
            stores.append(store)
    for store in stores:
        store.wait()


def call(body, outs, smem, flops, *args, hbm=(), held=(), scratch=(), manual=False):
    moved = sum(a.size * a.dtype.itemsize for a in [*args, *held, *outs])
    inputs = [pltpu.with_memory_space_constraint(a, pltpu.VMEM) for a in args[smem:]]
    spec = lambda space: pl.BlockSpec(memory_space=space)
    return pl.pallas_call(
        body,
        out_shape=[
            a if i in hbm else pltpu.VMEM(a.shape, a.dtype) for i, a in enumerate(outs)
        ],
        in_specs=[spec(pltpu.SMEM)] * smem
        + [spec(pltpu.VMEM)] * len(inputs)
        + [spec(pltpu.HBM)] * len(held),
        out_specs=[
            spec(pltpu.HBM if manual and i in hbm else pltpu.VMEM) for i in range(len(outs))
        ],
        scratch_shapes=scratch,
        compiler_params=pltpu.CompilerParams(vmem_limit_bytes=4 * 2**20),
        cost_estimate=pl.CostEstimate(flops=flops, bytes_accessed=moved, transcendentals=0),
    )(*args[:smem], *inputs, *[pltpu.with_memory_space_constraint(a, pltpu.HBM) for a in held])


def carried(chunks, place, count, reverse, beside, order, order_back):
    def swap(array, turn):
        return lax.ppermute(array, "seq", [(i, i ^ turn) for i in range(count)])

    def shift(array, by):
        step = -by if reverse else by
        moved = lax.ppermute(array, "seq", [(i, (i + step) % count) for i in range(count)])
        inside = place < count - by if reverse else place >= by
        return jnp.where(inside, moved, 0.0)

    got = [chunks[0]] + [swap(chunks[1 + j], t) for j, t in enumerate(order)]
    extra = beside()
    total = got[0] + got[1] + got[2] + got[3]
    outside = shift(total, GROUP)
    by = 1
    while by < count // GROUP - 1:
        outside = outside + shift(outside, by * GROUP)
        by *= 2
    own = lax.bitwise_and(place, GROUP - 1).astype(jnp.int32).reshape(1)
    results = call(
        functools.partial(spread_kernel, reverse, order, order_back),
        [jax.ShapeDtypeStruct(total.shape, F32)] * GROUP,
        1,
        0,
        own,
        outside,
        *got,
    )
    return [results[0]] + [swap(results[1 + j], t) for j, t in enumerate(order_back)], extra


def per_device(seq_count, head_count, queries, keys, values, out_grad, out_gain):
    layers, tok_rows, width = queries.shape
    heads = width // DH
    assert tok_rows == CH and heads == GROUP and seq_count % GROUP == 0
    assert 2 * layers <= 8
    place = lax.axis_index("seq")
    place_arg = lax.bitwise_and(place, GROUP - 1).astype(jnp.int32).reshape(1)
    wide = lambda dtype: jax.ShapeDtypeStruct((layers, CH, width), dtype)
    blocks = [jax.ShapeDtypeStruct((layers, DH, DH), F32)] * GROUP
    product = 2 * layers * heads * CH * DH * DH

    keys, values, *kv = call(
        functools.partial(kv_kernel, ORDERS[0]),
        [wide(BF16), wide(BF16), *blocks],
        1,
        product,
        place_arg,
        held=(keys, values),
        scratch=[pltpu.SemaphoreType.DMA((2, layers))],
    )
    queries, out_grad, kv = lax.optimization_barrier((queries, out_grad, kv))
    states, (weights, local) = carried(
        kv,
        place,
        seq_count,
        False,
        lambda: call(
            local_kernel, [wide(BF16), wide(F32)], 0, 2 * product, queries, keys, values
        ),
        ORDERS[0],
        ORDERS[1],
    )
    attn, s16, sums = call(
        functools.partial(attn_kernel, ORDERS[1]),
        [wide(F32), wide(BF16), jax.ShapeDtypeStruct((8, CH), F32)],
        1,
        product,
        place_arg,
        queries,
        local,
        out_grad,
        out_gain,
        *states,
    )
    def across(array, by):
        pairs = [(i, (i + by) % head_count) for i in range(head_count)]
        return lax.ppermute(array, "head", pairs)

    parts = [sums] + [across(sums, by) for by in range(head_count - 1, 0, -1)]
    ga, inv, *products = call(
        functools.partial(grad_kernel, width * head_count, ORDERS[2]),
        [wide(BF16), jax.ShapeDtypeStruct((layers, CH, DH), F32), *blocks],
        1,
        product,
        place_arg,
        attn,
        out_grad,
        out_gain,
        queries,
        *parts,
    )
    later, (normed, grad_q, gk_local, gv_local) = carried(
        products,
        place,
        seq_count,
        True,
        lambda: call(
            inner_kernel,
            [wide(BF16), wide(BF16), wide(F32), wide(F32)],
            0,
            5 * product,
            queries,
            keys,
            values,
            out_gain,
            attn,
            inv,
            ga,
            s16,
            weights,
            hbm=(0, 1),
        ),
        ORDERS[2],
        ORDERS[3],
    )
    tile = pltpu.VMEM(queries.shape, BF16)
    grad_k, grad_v = call(
        functools.partial(outer_kernel, ORDERS[3]),
        [wide(BF16), wide(BF16)],
        1,
        2 * product,
        place_arg,
        keys,
        values,
        gk_local,
        gv_local,
        *later,
        hbm=(0, 1),
        scratch=[tile, tile, pltpu.SemaphoreType.DMA((2, layers))],
        manual=True,
    )
    return normed, grad_q, grad_k, grad_v


def solution(mesh):
    block = P(None, "seq", "head")
    return jax.shard_map(
        functools.partial(per_device, mesh.shape["seq"], mesh.shape["head"]),
        mesh=mesh,
        in_specs=(block, block, block, block, P(None, "head")),
        out_specs=(block, block, block, block),
        check_vma=False,
    )
```

```python
import functools

import jax
import jax.numpy as jnp
from jax import lax
from jax.experimental import pallas as pl
from jax.experimental.pallas import tpu as pltpu
from jax.sharding import PartitionSpec as P

DH = 128
CH = 128
GROUP = 4
EARLY = 2
ORDERS = ((2, 1, 3), (3, 1, 2), (1, 3, 2), (3, 1, 2))

EPSILON = 1e-06
SCALE = DH ** (-0.5)
F32 = jnp.float32
BF16 = jnp.bfloat16


def dot(a, b, ca, cb):
    return lax.dot_general(a, b, (((ca,), (cb,)), ((), ())), preferred_element_type=F32)


def lanes(head):
    return pl.ds(pl.multiple_of(head * DH, DH), DH)


def causal_mask():
    rows = lax.broadcasted_iota(jnp.int32, (CH, CH), 0)
    cols = lax.broadcasted_iota(jnp.int32, (CH, CH), 1)
    return rows >= cols


def local_part(early, q_ref, k_ref, v_ref, w_ref, loc_ref):
    mask = causal_mask()
    layers, _, width = q_ref.shape
    every = [(layer, head) for layer in range(layers) for head in range(width // DH)]
    for layer, head in every[:EARLY] if early else every[EARLY:]:
        at = pl.ds(head * DH, DH)
        scores = dot(q_ref[layer, :, at], k_ref[layer, :, at], 1, 1) * SCALE
        w = jnp.where(mask, scores, 0.0).astype(BF16)
        w_ref[layer, :, at] = w
        loc_ref[layer, :, at] = dot(w, v_ref[layer, :, at], 1, 0)


def held_back():
    return lax.rem(lax.axis_index("head"), 2) == 0


def kv_kernel(order, place_ref, *refs):
    sources, (q_ref, k_ref, v_ref) = refs[:3], refs[3:6]
    w_ref, loc_ref = refs[6:8]
    outs, sems = refs[8:-1], refs[-1]
    loads = [
        [
            pltpu.make_async_copy(src.at[layer], dst.at[layer], sems.at[i, layer])
            for layer in range(k_ref.shape[0])
        ]
        for i, (src, dst) in enumerate(zip(sources, (q_ref, k_ref, v_ref)))
    ]
    for load in loads[1] + loads[2] + loads[0]:
        load.start()
    for load in loads[1] + loads[2]:
        load.wait()
    place = place_ref[0]
    for turn, out in zip((0, *order), outs):
        at = lanes(lax.bitwise_xor(place, turn))
        for layer in range(k_ref.shape[0]):
            out[layer] = dot(k_ref[layer, :, at], v_ref[layer, :, at], 0, 0)
    for load in loads[0]:
        load.wait()

    @pl.when(held_back())
    def _():
        local_part(True, q_ref, k_ref, v_ref, w_ref, loc_ref)


def local_kernel(q_ref, k_ref, v_ref, w_in, loc_in, w_ref, loc_ref):
    local_part(False, q_ref, k_ref, v_ref, w_ref, loc_ref)

    @pl.when(jnp.logical_not(held_back()))
    def _():
        local_part(True, q_ref, k_ref, v_ref, w_ref, loc_ref)


def spread_kernel(reverse, order, order_back, place_ref, outside_ref, *refs):
    got, outs = refs[:GROUP], refs[GROUP:]
    place = place_ref[0]
    for layer in range(outside_ref.shape[0]):
        for turn, out in zip((0, *order_back), outs):
            goal = lax.bitwise_xor(place, turn)
            value = outside_ref[layer]
            for t, ref in zip((0, *order), got):
                source = lax.bitwise_xor(place, t)
                reached = source > goal if reverse else source < goal
                value = value + jnp.where(reached, ref[layer], 0.0)
            out[layer] = value


def attn_kernel(order, place_ref, q_ref, loc_ref, g_ref, gain_ref, *rest):
    states, (attn_ref, s16_ref, sums_ref) = rest[:GROUP], rest[GROUP:]
    place = place_ref[0]
    layers = q_ref.shape[0]
    lane = lax.broadcasted_iota(jnp.int32, (CH, CH), 1)
    columns = jnp.zeros((CH, CH), F32)
    for layer in range(layers):
        square = jnp.zeros((CH, DH), F32)
        cross = jnp.zeros((CH, DH), F32)
        for turn, state in zip((0, *order), states):
            at = lanes(lax.bitwise_xor(place, turn))
            s16 = state[layer].astype(BF16)
            s16_ref[layer, :, at] = s16
            attn = SCALE * dot(q_ref[layer, :, at], s16, 1, 0) + loc_ref[layer, :, at]
            attn_ref[layer, :, at] = attn
            upper = gain_ref[layer : layer + 1, at] * g_ref[layer, :, at].astype(F32)
            square += attn * attn
            cross += upper * attn
        columns += jnp.where(lane == 2 * layer, jnp.sum(square, 1, keepdims=True), 0.0)
        columns += jnp.where(lane == 2 * layer + 1, jnp.sum(cross, 1, keepdims=True), 0.0)
    sums_ref[...] = columns.T[: sums_ref.shape[0]]


def grad_kernel(total_width, order, place_ref, attn_ref, g_ref, gain_ref, q_ref, *rest):
    parts = rest[: len(rest) - GROUP - 2]
    ga_ref, inv_ref = rest[len(parts) : len(parts) + 2]
    outs = rest[len(parts) + 2 :]
    place = place_ref[0]
    layers = attn_ref.shape[0]
    sums = parts[0][...]
    for part in parts[1:]:
        sums = sums + part[...]
    sums = jnp.concatenate([sums, jnp.zeros((CH - sums.shape[0], CH), F32)], 0).T
    for layer in range(layers):
        square = sums[:, 2 * layer : 2 * layer + 1] * (1.0 / total_width)
        cross = sums[:, 2 * layer + 1 : 2 * layer + 2] * (1.0 / total_width)
        inv = 1.0 / jnp.sqrt(square + EPSILON)
        back = cross * (inv * inv * inv)
        inv_ref[layer] = jnp.broadcast_to(inv, inv_ref.shape[1:])
        for turn, out in zip((0, *order), outs):
            at = lanes(lax.bitwise_xor(place, turn))
            upper = gain_ref[layer : layer + 1, at] * g_ref[layer, :, at].astype(F32)
            ga = (upper * inv - attn_ref[layer, :, at] * back).astype(BF16)
            ga_ref[layer, :, at] = ga
            out[layer] = dot(q_ref[layer, :, at], ga, 0, 0)


def inner_kernel(q_ref, k_ref, v_ref, gain_ref, attn_ref, inv_ref, *rest):
    ga_ref, s16_ref, w_ref, normed_ref, gq_ref, gkl_ref, gvl_ref = rest
    mask = causal_mask()
    layers, _, width = q_ref.shape
    for layer in range(layers):
        for head in range(width // DH):
            at = pl.ds(head * DH, DH)
            gain = gain_ref[layer : layer + 1, at]
            normed_ref[layer, :, at] = (attn_ref[layer, :, at] * inv_ref[layer] * gain).astype(BF16)
            ga = ga_ref[layer, :, at]
            dscores = dot(ga, v_ref[layer, :, at], 1, 1) * SCALE
            dw = jnp.where(mask, dscores, 0.0).astype(BF16)
            gq = SCALE * dot(ga, s16_ref[layer, :, at], 1, 1)
            gq_ref[layer, :, at] = (gq + dot(dw, k_ref[layer, :, at], 1, 0)).astype(BF16)
            gkl_ref[layer, :, at] = dot(dw, q_ref[layer, :, at], 0, 0)
            gvl_ref[layer, :, at] = dot(w_ref[layer, :, at], ga, 0, 0)


def outer_kernel(order, place_ref, k_ref, v_ref, gkl_ref, gvl_ref, *rest):
    backs, (gk_hbm, gv_hbm, gk_ref, gv_ref, sems) = rest[:GROUP], rest[GROUP:]
    place = place_ref[0]
    stores = []
    for layer in range(k_ref.shape[0]):
        for turn, back in zip((0, *order), backs):
            at = lanes(lax.bitwise_xor(place, turn))
            b16 = (SCALE * back[layer]).astype(BF16)
            gk = dot(v_ref[layer, :, at], b16, 1, 1) + gkl_ref[layer, :, at]
            gv = dot(k_ref[layer, :, at], b16, 1, 0) + gvl_ref[layer, :, at]
            gk_ref[layer, :, at] = gk.astype(BF16)
            gv_ref[layer, :, at] = gv.astype(BF16)
        for i, (src, dst) in enumerate(((gk_ref, gk_hbm), (gv_ref, gv_hbm))):
            store = pltpu.make_async_copy(src.at[layer], dst.at[layer], sems.at[i, layer])
            store.start()
            stores.append(store)
    for store in stores:
        store.wait()


def call(body, outs, smem, flops, *args, hbm=(), held=(), scratch=(), manual=False, alias={}):
    moved = sum(a.size * a.dtype.itemsize for a in [*args, *held, *outs])
    inputs = [pltpu.with_memory_space_constraint(a, pltpu.VMEM) for a in args[smem:]]
    spec = lambda space: pl.BlockSpec(memory_space=space)
    return pl.pallas_call(
        body,
        out_shape=[
            a if i in hbm else pltpu.VMEM(a.shape, a.dtype) for i, a in enumerate(outs)
        ],
        in_specs=[spec(pltpu.SMEM)] * smem
        + [spec(pltpu.VMEM)] * len(inputs)
        + [spec(pltpu.HBM)] * len(held),
        out_specs=[
            spec(pltpu.HBM if manual and i in hbm else pltpu.VMEM) for i in range(len(outs))
        ],
        scratch_shapes=scratch,
        input_output_aliases=alias,
        compiler_params=pltpu.CompilerParams(vmem_limit_bytes=4 * 2**20),
        cost_estimate=pl.CostEstimate(flops=flops, bytes_accessed=moved, transcendentals=0),
    )(*args[:smem], *inputs, *[pltpu.with_memory_space_constraint(a, pltpu.HBM) for a in held])


def carried(chunks, place, count, reverse, beside, order, order_back):
    def swap(array, turn):
        return lax.ppermute(array, "seq", [(i, i ^ turn) for i in range(count)])

    def shift(array, by):
        step = -by if reverse else by
        moved = lax.ppermute(array, "seq", [(i, (i + step) % count) for i in range(count)])
        inside = place < count - by if reverse else place >= by
        return jnp.where(inside, moved, 0.0)

    got = [chunks[0]] + [swap(chunks[1 + j], t) for j, t in enumerate(order)]
    extra = beside()
    total = got[0] + got[1] + got[2] + got[3]
    outside = shift(total, GROUP)
    by = 1
    while by < count // GROUP - 1:
        outside = outside + shift(outside, by * GROUP)
        by *= 2
    own = lax.bitwise_and(place, GROUP - 1).astype(jnp.int32).reshape(1)
    results = call(
        functools.partial(spread_kernel, reverse, order, order_back),
        [jax.ShapeDtypeStruct(total.shape, F32)] * GROUP,
        1,
        0,
        own,
        outside,
        *got,
    )
    return [results[0]] + [swap(results[1 + j], t) for j, t in enumerate(order_back)], extra


def per_device(seq_count, head_count, queries, keys, values, out_grad, out_gain):
    layers, tok_rows, width = queries.shape
    heads = width // DH
    assert tok_rows == CH and heads == GROUP and seq_count % GROUP == 0
    assert 2 * layers <= 8
    place = lax.axis_index("seq")
    place_arg = lax.bitwise_and(place, GROUP - 1).astype(jnp.int32).reshape(1)
    wide = lambda dtype: jax.ShapeDtypeStruct((layers, CH, width), dtype)
    blocks = [jax.ShapeDtypeStruct((layers, DH, DH), F32)] * GROUP
    product = 2 * layers * heads * CH * DH * DH

    queries, keys, values, weights, local, *kv = call(
        functools.partial(kv_kernel, ORDERS[0]),
        [wide(BF16)] * 4 + [wide(F32), *blocks],
        1,
        3 * product,
        place_arg,
        held=(queries, keys, values),
        scratch=[pltpu.SemaphoreType.DMA((3, layers))],
    )
    out_grad, kv = lax.optimization_barrier((out_grad, kv))
    states, (weights, local) = carried(
        kv,
        place,
        seq_count,
        False,
        lambda: call(
            local_kernel,
            [wide(BF16), wide(F32)],
            0,
            2 * product,
            queries,
            keys,
            values,
            weights,
            local,
            alias={3: 0, 4: 1},
        ),
        ORDERS[0],
        ORDERS[1],
    )
    attn, s16, sums = call(
        functools.partial(attn_kernel, ORDERS[1]),
        [wide(F32), wide(BF16), jax.ShapeDtypeStruct((8, CH), F32)],
        1,
        product,
        place_arg,
        queries,
        local,
        out_grad,
        out_gain,
        *states,
    )
    def across(array, by):
        pairs = [(i, (i + by) % head_count) for i in range(head_count)]
        return lax.ppermute(array, "head", pairs)

    parts = [sums] + [across(sums, by) for by in range(head_count - 1, 0, -1)]
    ga, inv, *products = call(
        functools.partial(grad_kernel, width * head_count, ORDERS[2]),
        [wide(BF16), jax.ShapeDtypeStruct((layers, CH, DH), F32), *blocks],
        1,
        product,
        place_arg,
        attn,
        out_grad,
        out_gain,
        queries,
        *parts,
    )
    later, (normed, grad_q, gk_local, gv_local) = carried(
        products,
        place,
        seq_count,
        True,
        lambda: call(
            inner_kernel,
            [wide(BF16), wide(BF16), wide(F32), wide(F32)],
            0,
            5 * product,
            queries,
            keys,
            values,
            out_gain,
            attn,
            inv,
            ga,
            s16,
            weights,
            hbm=(0, 1),
        ),
        ORDERS[2],
        ORDERS[3],
    )
    tile = pltpu.VMEM((layers, CH, width), BF16)
    grad_k, grad_v = call(
        functools.partial(outer_kernel, ORDERS[3]),
        [wide(BF16), wide(BF16)],
        1,
        2 * product,
        place_arg,
        keys,
        values,
        gk_local,
        gv_local,
        *later,
        hbm=(0, 1),
        scratch=[tile, tile, pltpu.SemaphoreType.DMA((2, layers))],
        manual=True,
    )
    return normed, grad_q, grad_k, grad_v


def solution(mesh):
    block = P(None, "seq", "head")
    return jax.shard_map(
        functools.partial(per_device, mesh.shape["seq"], mesh.shape["head"]),
        mesh=mesh,
        in_specs=(block, block, block, block, P(None, "head")),
        out_specs=(block, block, block, block),
        check_vma=False,
    )
```

```python
import functools

import jax
import jax.numpy as jnp
from jax import lax
from jax.experimental import pallas as pl
from jax.experimental.pallas import tpu as pltpu
from jax.sharding import PartitionSpec as P

DH = 128
CH = 128
GROUP = 4
EARLY = 2
ORDERS = ((2, 1, 3), (3, 1, 2), (3, 2, 1), (3, 1, 2))

EPSILON = 1e-06
SCALE = DH ** (-0.5)
F32 = jnp.float32
BF16 = jnp.bfloat16


def dot(a, b, ca, cb):
    return lax.dot_general(a, b, (((ca,), (cb,)), ((), ())), preferred_element_type=F32)


def lanes(head):
    return pl.ds(pl.multiple_of(head * DH, DH), DH)


def causal_mask():
    rows = lax.broadcasted_iota(jnp.int32, (CH, CH), 0)
    cols = lax.broadcasted_iota(jnp.int32, (CH, CH), 1)
    return rows >= cols


def local_part(early, q_ref, k_ref, v_ref, w_ref, loc_ref):
    mask = causal_mask()
    layers, _, width = q_ref.shape
    every = [(layer, head) for layer in range(layers) for head in range(width // DH)]
    for layer, head in every[:EARLY] if early else every[EARLY:]:
        at = pl.ds(head * DH, DH)
        scores = dot(q_ref[layer, :, at], k_ref[layer, :, at], 1, 1) * SCALE
        w = jnp.where(mask, scores, 0.0).astype(BF16)
        w_ref[layer, :, at] = w
        loc_ref[layer, :, at] = dot(w, v_ref[layer, :, at], 1, 0)


def held_back():
    return lax.rem(lax.axis_index("head"), 2) == 0


def kv_kernel(order, place_ref, *refs):
    sources, (q_ref, k_ref, v_ref) = refs[:3], refs[3:6]
    w_ref, loc_ref = refs[6:8]
    outs, sems = refs[8:-1], refs[-1]
    loads = [
        [
            pltpu.make_async_copy(src.at[layer], dst.at[layer], sems.at[i, layer])
            for layer in range(k_ref.shape[0])
        ]
        for i, (src, dst) in enumerate(zip(sources, (q_ref, k_ref, v_ref)))
    ]
    for load in loads[1] + loads[2] + loads[0]:
        load.start()
    for load in loads[1] + loads[2]:
        load.wait()
    place = place_ref[0]
    for turn, out in zip((0, *order), outs):
        at = lanes(lax.bitwise_xor(place, turn))
        for layer in range(k_ref.shape[0]):
            out[layer] = dot(k_ref[layer, :, at], v_ref[layer, :, at], 0, 0)
    for load in loads[0]:
        load.wait()

    @pl.when(held_back())
    def _():
        local_part(True, q_ref, k_ref, v_ref, w_ref, loc_ref)


def local_kernel(q_ref, k_ref, v_ref, w_in, loc_in, w_ref, loc_ref):
    local_part(False, q_ref, k_ref, v_ref, w_ref, loc_ref)

    @pl.when(jnp.logical_not(held_back()))
    def _():
        local_part(True, q_ref, k_ref, v_ref, w_ref, loc_ref)


def spread_kernel(reverse, order, order_back, place_ref, outside_ref, *refs):
    got, outs = refs[:GROUP], refs[GROUP:]
    place = place_ref[0]
    for layer in range(outside_ref.shape[0]):
        for turn, out in zip((0, *order_back), outs):
            goal = lax.bitwise_xor(place, turn)
            value = outside_ref[layer]
            for t, ref in zip((0, *order), got):
                source = lax.bitwise_xor(place, t)
                reached = source > goal if reverse else source < goal
                value = value + jnp.where(reached, ref[layer], 0.0)
            out[layer] = value


def attn_kernel(order, place_ref, q_ref, loc_ref, g_ref, gain_ref, *rest):
    states, (attn_ref, s16_ref, sums_ref) = rest[:GROUP], rest[GROUP:]
    place = place_ref[0]
    layers = q_ref.shape[0]
    lane = lax.broadcasted_iota(jnp.int32, (CH, CH), 1)
    columns = jnp.zeros((CH, CH), F32)
    for layer in range(layers):
        square = jnp.zeros((CH, DH), F32)
        cross = jnp.zeros((CH, DH), F32)
        for turn, state in zip((0, *order), states):
            at = lanes(lax.bitwise_xor(place, turn))
            s16 = state[layer].astype(BF16)
            s16_ref[layer, :, at] = s16
            attn = SCALE * dot(q_ref[layer, :, at], s16, 1, 0) + loc_ref[layer, :, at]
            attn_ref[layer, :, at] = attn
            upper = gain_ref[layer : layer + 1, at] * g_ref[layer, :, at].astype(F32)
            square += attn * attn
            cross += upper * attn
        columns += jnp.where(lane == 2 * layer, jnp.sum(square, 1, keepdims=True), 0.0)
        columns += jnp.where(lane == 2 * layer + 1, jnp.sum(cross, 1, keepdims=True), 0.0)
    sums_ref[...] = columns.T[: sums_ref.shape[0]]


def grad_kernel(total_width, order, place_ref, attn_ref, g_ref, gain_ref, q_ref, *rest):
    parts = rest[: len(rest) - GROUP - 2]
    ga_ref, inv_ref = rest[len(parts) : len(parts) + 2]
    outs = rest[len(parts) + 2 :]
    place = place_ref[0]
    layers = attn_ref.shape[0]
    sums = parts[0][...]
    for part in parts[1:]:
        sums = sums + part[...]
    sums = jnp.concatenate([sums, jnp.zeros((CH - sums.shape[0], CH), F32)], 0).T
    for layer in range(layers):
        square = sums[:, 2 * layer : 2 * layer + 1] * (1.0 / total_width)
        cross = sums[:, 2 * layer + 1 : 2 * layer + 2] * (1.0 / total_width)
        inv = 1.0 / jnp.sqrt(square + EPSILON)
        back = cross * (inv * inv * inv)
        inv_ref[layer] = jnp.broadcast_to(inv, inv_ref.shape[1:])
        for turn, out in zip((0, *order), outs):
            at = lanes(lax.bitwise_xor(place, turn))
            upper = gain_ref[layer : layer + 1, at] * g_ref[layer, :, at].astype(F32)
            ga = (upper * inv - attn_ref[layer, :, at] * back).astype(BF16)
            ga_ref[layer, :, at] = ga
            out[layer] = dot(q_ref[layer, :, at], ga, 0, 0)


def inner_kernel(q_ref, k_ref, v_ref, gain_ref, attn_ref, inv_ref, *rest):
    ga_ref, s16_ref, w_ref, normed_ref, gq_ref, gkl_ref, gvl_ref = rest
    mask = causal_mask()
    layers, _, width = q_ref.shape
    for layer in range(layers):
        for head in range(width // DH):
            at = pl.ds(head * DH, DH)
            gain = gain_ref[layer : layer + 1, at]
            normed_ref[layer, :, at] = (attn_ref[layer, :, at] * inv_ref[layer] * gain).astype(BF16)
            ga = ga_ref[layer, :, at]
            dscores = dot(ga, v_ref[layer, :, at], 1, 1) * SCALE
            dw = jnp.where(mask, dscores, 0.0).astype(BF16)
            gq = SCALE * dot(ga, s16_ref[layer, :, at], 1, 1)
            gq_ref[layer, :, at] = (gq + dot(dw, k_ref[layer, :, at], 1, 0)).astype(BF16)
            gkl_ref[layer, :, at] = dot(dw, q_ref[layer, :, at], 0, 0)
            gvl_ref[layer, :, at] = dot(w_ref[layer, :, at], ga, 0, 0)


def outer_kernel(order, place_ref, k_ref, v_ref, gkl_ref, gvl_ref, *rest):
    backs, (gk_hbm, gv_hbm, gk_ref, gv_ref, sems) = rest[:GROUP], rest[GROUP:]
    place = place_ref[0]
    stores = []
    for layer in range(k_ref.shape[0]):
        for turn, back in zip((0, *order), backs):
            at = lanes(lax.bitwise_xor(place, turn))
            b16 = (SCALE * back[layer]).astype(BF16)
            gk = dot(v_ref[layer, :, at], b16, 1, 1) + gkl_ref[layer, :, at]
            gv = dot(k_ref[layer, :, at], b16, 1, 0) + gvl_ref[layer, :, at]
            gk_ref[layer, :, at] = gk.astype(BF16)
            gv_ref[layer, :, at] = gv.astype(BF16)
        for i, (src, dst) in enumerate(((gk_ref, gk_hbm), (gv_ref, gv_hbm))):
            store = pltpu.make_async_copy(src.at[layer], dst.at[layer], sems.at[i, layer])
            store.start()
            stores.append(store)
    for store in stores:
        store.wait()


def call(body, outs, smem, flops, *args, hbm=(), held=(), scratch=(), manual=False, alias={}):
    moved = sum(a.size * a.dtype.itemsize for a in [*args, *held, *outs])
    inputs = [pltpu.with_memory_space_constraint(a, pltpu.VMEM) for a in args[smem:]]
    spec = lambda space: pl.BlockSpec(memory_space=space)
    return pl.pallas_call(
        body,
        out_shape=[
            a if i in hbm else pltpu.VMEM(a.shape, a.dtype) for i, a in enumerate(outs)
        ],
        in_specs=[spec(pltpu.SMEM)] * smem
        + [spec(pltpu.VMEM)] * len(inputs)
        + [spec(pltpu.HBM)] * len(held),
        out_specs=[
            spec(pltpu.HBM if manual and i in hbm else pltpu.VMEM) for i in range(len(outs))
        ],
        scratch_shapes=scratch,
        input_output_aliases=alias,
        compiler_params=pltpu.CompilerParams(vmem_limit_bytes=4 * 2**20),
        cost_estimate=pl.CostEstimate(flops=flops, bytes_accessed=moved, transcendentals=0),
    )(*args[:smem], *inputs, *[pltpu.with_memory_space_constraint(a, pltpu.HBM) for a in held])


def carried(chunks, place, count, reverse, beside, order, order_back):
    def swap(array, turn):
        return lax.ppermute(array, "seq", [(i, i ^ turn) for i in range(count)])

    def shift(array, by):
        step = -by if reverse else by
        moved = lax.ppermute(array, "seq", [(i, (i + step) % count) for i in range(count)])
        inside = place < count - by if reverse else place >= by
        return jnp.where(inside, moved, 0.0)

    got = [chunks[0]] + [swap(chunks[1 + j], t) for j, t in enumerate(order)]
    extra = beside()
    total = got[0] + got[1] + got[2] + got[3]
    outside = shift(total, GROUP)
    by = 1
    while by < count // GROUP - 1:
        outside = outside + shift(outside, by * GROUP)
        by *= 2
    own = lax.bitwise_and(place, GROUP - 1).astype(jnp.int32).reshape(1)
    results = call(
        functools.partial(spread_kernel, reverse, order, order_back),
        [jax.ShapeDtypeStruct(total.shape, F32)] * GROUP,
        1,
        0,
        own,
        outside,
        *got,
    )
    return [results[0]] + [swap(results[1 + j], t) for j, t in enumerate(order_back)], extra


def per_device(seq_count, head_count, queries, keys, values, out_grad, out_gain):
    layers, tok_rows, width = queries.shape
    heads = width // DH
    assert tok_rows == CH and heads == GROUP and seq_count % GROUP == 0
    assert 2 * layers <= 8
    place = lax.axis_index("seq")
    place_arg = lax.bitwise_and(place, GROUP - 1).astype(jnp.int32).reshape(1)
    wide = lambda dtype: jax.ShapeDtypeStruct((layers, CH, width), dtype)
    blocks = [jax.ShapeDtypeStruct((layers, DH, DH), F32)] * GROUP
    product = 2 * layers * heads * CH * DH * DH

    queries, keys, values, weights, local, *kv = call(
        functools.partial(kv_kernel, ORDERS[0]),
        [wide(BF16)] * 4 + [wide(F32), *blocks],
        1,
        3 * product,
        place_arg,
        held=(queries, keys, values),
        scratch=[pltpu.SemaphoreType.DMA((3, layers))],
    )
    out_grad, kv = lax.optimization_barrier((out_grad, kv))
    states, (weights, local) = carried(
        kv,
        place,
        seq_count,
        False,
        lambda: call(
            local_kernel,
            [wide(BF16), wide(F32)],
            0,
            2 * product,
            queries,
            keys,
            values,
            weights,
            local,
            alias={3: 0, 4: 1},
        ),
        ORDERS[0],
        ORDERS[1],
    )
    attn, s16, sums = call(
        functools.partial(attn_kernel, ORDERS[1]),
        [wide(F32), wide(BF16), jax.ShapeDtypeStruct((8, CH), F32)],
        1,
        product,
        place_arg,
        queries,
        local,
        out_grad,
        out_gain,
        *states,
    )
    def across(array, by):
        pairs = [(i, (i + by) % head_count) for i in range(head_count)]
        return lax.ppermute(array, "head", pairs)

    parts = [sums] + [across(sums, by) for by in range(head_count - 1, 0, -1)]
    ga, inv, *products = call(
        functools.partial(grad_kernel, width * head_count, ORDERS[2]),
        [wide(BF16), jax.ShapeDtypeStruct((layers, CH, DH), F32), *blocks],
        1,
        product,
        place_arg,
        attn,
        out_grad,
        out_gain,
        queries,
        *parts,
    )
    later, (normed, grad_q, gk_local, gv_local) = carried(
        products,
        place,
        seq_count,
        True,
        lambda: call(
            inner_kernel,
            [wide(BF16), wide(BF16), wide(F32), wide(F32)],
            0,
            5 * product,
            queries,
            keys,
            values,
            out_gain,
            attn,
            inv,
            ga,
            s16,
            weights,
            hbm=(0, 1),
        ),
        ORDERS[2],
        ORDERS[3],
    )
    tile = pltpu.VMEM((layers, CH, width), BF16)
    grad_k, grad_v = call(
        functools.partial(outer_kernel, ORDERS[3]),
        [wide(BF16), wide(BF16)],
        1,
        2 * product,
        place_arg,
        keys,
        values,
        gk_local,
        gv_local,
        *later,
        hbm=(0, 1),
        scratch=[tile, tile, pltpu.SemaphoreType.DMA((2, layers))],
        manual=True,
    )
    return normed, grad_q, grad_k, grad_v


def solution(mesh):
    block = P(None, "seq", "head")
    return jax.shard_map(
        functools.partial(per_device, mesh.shape["seq"], mesh.shape["head"]),
        mesh=mesh,
        in_specs=(block, block, block, block, P(None, "head")),
        out_specs=(block, block, block, block),
        check_vma=False,
    )
```
